32 devices in a mesh: seq: 4 (over y, core), fsdp: 8 (over z, x).
Axes of the slice: x: 2, y: 2, z: 4, core: 2. Of those that a mesh axis runs over, the one named last changes fastest.
Arguments:
- tokens: bfloat16 [2, 8, 256, 1536], P(None, 'fsdp', 'seq'), may hold values from -6 to 6
- segments: int32 [2, 8, 256], P(None, 'fsdp'), may hold values from 0 to 3, never falling along the last dimension, each value on 1 to 128 neighbouring positions
- routes: int32 [2, 8, 256, 2], P(None, 'fsdp'), may hold values from 0 to 3, all different within a row; in each aligned block of 64 rows (0 to 63, 64 to 127, ..., all dimensions but the last counted through in order) at most 48 rows name the same one
- cotangent: bfloat16 [2, 8, 256, 1536], P(None, 'fsdp', 'seq'), may hold values from -6 to 6
- norm1: bfloat16 [1536], P('fsdp'), may hold values from 0.25 to 1.75
- w_query: bfloat16 [1536, 1536], P('fsdp', 'seq'), may hold values from -0.15625 to 0.15625
- w_key: bfloat16 [1536, 512], P('fsdp', 'seq'), may hold values from -0.15625 to 0.15625
- w_value: bfloat16 [1536, 512], P('fsdp', 'seq'), may hold values from -0.15625 to 0.15625
- w_out: bfloat16 [1536, 1536], P('seq', 'fsdp'), may hold values from -0.875 to 0.875
- norm2: bfloat16 [1536], P('fsdp'), may hold values from 0.25 to 1.75
- w_router: bfloat16 [1536, 4], P('fsdp'), may hold values from -0.21875 to 0.21875
- w_gate: bfloat16 [4, 1536, 1024], P(None, 'fsdp', 'seq'), may hold values from -0.15625 to 0.15625
- w_up: bfloat16 [4, 1536, 1024], P(None, 'fsdp', 'seq'), may hold values from -0.15625 to 0.15625
- w_down: bfloat16 [4, 1024, 1536], P(None, 'seq', 'fsdp'), may hold values from -0.1875 to 0.1875
Outputs:
- layer_out: bfloat16 [2, 8, 256, 1536], P(None, 'fsdp', 'seq')
- grad_input: float32 [2, 8, 256, 1536], P(None, 'fsdp', 'seq')
- grad_norm1: float32 [1536], P('fsdp')
- grad_query: float32 [1536, 1536], P('fsdp', 'seq')
- grad_key: float32 [1536, 512], P('fsdp', 'seq')
- grad_value: float32 [1536, 512], P('fsdp', 'seq')
- grad_out: float32 [1536, 1536], P('seq', 'fsdp')
- grad_norm2: float32 [1536], P('fsdp')
- grad_router: float32 [1536, 4], P('fsdp')
- grad_gate: float32 [4, 1536, 1024], P(None, 'fsdp', 'seq')
- grad_up: float32 [4, 1536, 1024], P(None, 'fsdp', 'seq')
- grad_down: float32 [4, 1024, 1536], P(None, 'seq', 'fsdp')
The draws below stay inside these ranges and needn't reach their ends.
Inputs may be any that keep to these rules, and one draw needn't show every extreme that they name: `segments`: each sequence's ids never fall; each of the 4 ids has 1 to 128 positions, and one has exactly 128. `routes`: A token's two experts differ. Within the rows of one device (aligned blocks of 64 rows in the order micro-batch, sequence, position) no expert is named by more than 48 rows, and in some block one is named by exactly 48.
All inputs are finite; a program needn't handle non-finite values.
Results may differ from the reference program's by a relative error of at most 0.02.
Values may be sent and summed in bfloat16 or wider, within the bound.
No kernel may reach another device: no remote copies, remote signals or barrier semaphores. Data moves between devices by JAX's collectives and lax.ppermute only.
A program may use at most 320 MiB of HBM per device.

```python
import math
import jax
import jax.numpy as jnp
import numpy as np
from jax import lax

D = 1536
HEADS = 24
HEAD_DIM = 64
KV_HEADS = 8
FF = 1024
EXPERTS = 4
TOP = 2
TOK_DEV = 64
MICRO = 2
DOCS = 4
CAP = 48
LEN = 256
SEQS = 8


def block_levels(stream_key, shape, cuts, smallest, high):
    level = 1.0
    for axis_at, shards_of in cuts:
        steps = jax.random.uniform(jax.random.fold_in(jax.random.fold_in(stream_key, 6), axis_at), (shards_of,), jnp.float32, smallest / len(cuts), high / len(cuts))
        level = level * jnp.repeat(jnp.exp(steps), shape[axis_at] // shards_of).reshape((-1,) + (1,) * (len(shape) - 1 - axis_at))
    return level


def split_up(count, total, bound, slope):
    weights = [(1 << 20) // math.isqrt(standing ** slope) + 1 for standing in range(2, count + 1)]
    surplus, holding = total - bound - (count - 1), [1] * (count - 1)
    while surplus > 0:
        candidates = [i for i in range(count - 1) if holding[i] < bound]
        pool, budget = sum([weights[i] for i in candidates]), surplus
        for i in candidates:
            more = min(bound - holding[i], max(1, budget * weights[i] // pool), surplus)
            holding[i] = holding[i] + more
            surplus = surplus - more
    return np.array([bound] + holding)


def ragged_sizes(own_key, count, total, reach, lean):
    if count == 2:
        one = jax.random.randint(own_key, (), max(1, total - reach), min(reach, total - 1) + 1)
        return jnp.stack([one, total - one])
    sizes = jnp.asarray(split_up(count, total, reach, lean), jnp.int32)
    pairs = (count - 1) // 2
    donor, taker = sizes[1:1 + 2 * pairs:2], sizes[2:2 + 2 * pairs:2]
    margin = jnp.minimum(donor - 1, reach - taker)
    moved = jax.random.randint(jax.random.fold_in(own_key, 1), (pairs,), 0, 1 << 20) % (margin + 1)
    sizes = sizes.at[1:1 + 2 * pairs:2].set(donor - moved).at[2:2 + 2 * pairs:2].set(taker + moved)
    return sizes[jax.random.permutation(jax.random.fold_in(own_key, 2), count)]


def routed_block(own_key, own, number, rows, count, top, limit, skew):
    sequence = jax.random.permutation(own_key, count)
    heavy_load, ordinary = shares(count, rows * top, limit, skew, True), shares(count, rows * top, limit, skew, False)
    places = jnp.arange(count)

    def named(sizes, rotation):
        used = int((sizes > 0).sum())
        fixed = max(1, used // 4)
        shifted = fixed + (places - fixed + rotation * (used - fixed)) % max(1, count - fixed)
        return jnp.zeros((count,), jnp.int32).at[sequence[jnp.where(places < fixed, places, shifted)]].set(jnp.asarray(sizes, jnp.int32))

    sizes = jnp.where(number % 4 == 0, named(heavy_load, number // 4), named(ordinary, number - number // 4 - 1))
    mixed = jax.random.permutation(jax.random.fold_in(own, 3), count)
    donor, taker = mixed[0:count // 2 * 2:2], mixed[1:count // 2 * 2:2]
    margin = jnp.minimum(sizes[donor] - 1, limit - sizes[taker]) // 2
    margin = jnp.where((donor == sequence[0]) | (taker == sequence[0]) | (sizes[taker] == 0), 0, jnp.maximum(margin, 0))
    shifted = jax.random.randint(jax.random.fold_in(own, 4), (count // 2,), 0, 1 << 20) % (margin + 1)
    sizes = sizes.at[donor].add(-shifted).at[taker].add(shifted)
    labels = jnp.searchsorted(jnp.cumsum(sizes), jnp.arange(rows * top), side="right").astype(jnp.int32)
    listing = labels.reshape(top, rows).T
    listing = listing[jax.random.permutation(jax.random.fold_in(own, 1), rows)]
    rotation = jax.random.randint(jax.random.fold_in(own, 2), (rows, 1), 0, top)
    return jnp.take_along_axis(listing, (jnp.arange(top)[None, :] + rotation) % top, axis=1)


def shares(amount, total, bound, lean, full):
    weights = [(1 << 20) // math.isqrt(grade ** lean) + 1 for grade in range(1, amount + 1)]
    largest = bound if full else min(bound, max(-(-total // amount), total * weights[0] // sum(weights)))
    least = 1 if total - largest >= amount - 1 else 0
    given, rest = [largest] + [least] * (amount - 1), total - largest - least * (amount - 1)
    while rest > 0:
        free = [i for i in range(1, amount) if given[i] < largest] or [i for i in range(1, amount) if given[i] < bound]
        whole, budget = sum([weights[i] for i in free]), rest
        for i in free:
            more = min(bound - given[i], max(1, budget * weights[i] // whole), rest)
            given[i] = given[i] + more
            rest = rest - more
    return np.array(given)


def noise(own_key, dims, width, bound, cuts=(), kind=jnp.bfloat16):
    drawn = width * jax.random.normal(own_key, dims, jnp.float32)
    if cuts:
        drawn = drawn * block_levels(own_key, dims, cuts, -0.22, 0.18)
    return jnp.clip(drawn, -bound, bound).astype(kind)


def setup_inputs(seed: int = 0) -> dict:
    splits = jax.random.split(jax.random.key(seed), 15)
    tokens = noise(splits[0], (MICRO, SEQS, LEN, D), 1.0, 6.0, ((1, 8), (2, 4)))
    segments = jax.vmap(lambda own: jnp.searchsorted(jnp.cumsum(ragged_sizes(own, DOCS, LEN, LEN // 2, 0)), jnp.arange(LEN), side="right"))(jax.random.split(splits[1], MICRO * SEQS)).reshape((MICRO, SEQS, LEN)).astype(jnp.int32)
    routes_keys = jax.random.split(jax.random.fold_in(splits[2], 1), MICRO * SEQS * LEN // TOK_DEV)
    routes_turns = jax.random.permutation(jax.random.fold_in(splits[2], 3), MICRO * SEQS * LEN // TOK_DEV)
    routes = jax.vmap(lambda own, number: routed_block(jax.random.fold_in(splits[2], 2), own, number, TOK_DEV, EXPERTS, TOP, CAP, 1))(routes_keys, routes_turns).reshape((MICRO, SEQS, LEN, TOP))
    cotangent = noise(splits[3], (MICRO, SEQS, LEN, D), 1.0, 6.0, ((1, 8), (2, 4)))
    norm1 = jnp.clip(1.0 + 0.15 * jax.random.normal(splits[4], (D,), jnp.float32), 0.25, 1.75).astype(jnp.bfloat16)
    w_query = noise(splits[5], (D, D), D ** -0.5, 0.15625, ((0, 8), (1, 4)))
    w_key = noise(splits[6], (D, KV_HEADS * HEAD_DIM), D ** -0.5, 0.15625, ((0, 8), (1, 4)))
    w_value = noise(splits[7], (D, KV_HEADS * HEAD_DIM), D ** -0.5, 0.15625, ((0, 8), (1, 4)))
    w_out = noise(splits[8], (D, D), (D // 32) ** -0.5, 0.875, ((0, 4), (1, 8)))
    norm2 = jnp.clip(1.0 + 0.15 * jax.random.normal(splits[9], (D,), jnp.float32), 0.25, 1.75).astype(jnp.bfloat16)
    w_router = noise(splits[10], (D, EXPERTS), (D // 2) ** -0.5, 0.21875, ((0, 8),))
    w_gate = noise(splits[11], (EXPERTS, D, FF), D ** -0.5, 0.15625, ((1, 8), (2, 4)))
    w_up = noise(splits[12], (EXPERTS, D, FF), D ** -0.5, 0.15625, ((1, 8), (2, 4)))
    w_down = noise(splits[13], (EXPERTS, FF, D), FF ** -0.5, 0.1875, ((1, 4), (2, 8)))
    return {"tokens": tokens, "segments": segments, "routes": routes, "cotangent": cotangent, "norm1": norm1, "w_query": w_query, "w_key": w_key, "w_value": w_value, "w_out": w_out, "norm2": norm2, "w_router": w_router, "w_gate": w_gate, "w_up": w_up, "w_down": w_down}


@jax.custom_vjp
def low(v):
    return lax.optimization_barrier(v.astype(jnp.bfloat16)).astype(jnp.float32)

@jax.custom_vjp
def low_back(v):
    return v

def low_keep(v):
    return (low(v), None)

def low_pass(kept, grad):
    return (grad,)

def back_keep(v):
    return (v, None)

def back_low(kept, grad):
    return (low(grad),)
low.defvjp(low_keep, low_pass)
low_back.defvjp(back_keep, back_low)
HIGH = lax.Precision.HIGHEST
EPS = 1e-05
NEG = -1e+30

def matmul(left_side, right_side):
    return jnp.dot(left_side, right_side, precision=HIGH, preferred_element_type=jnp.float32)

def rms_norm(values, gain):
    factor = lax.rsqrt(lax.optimization_barrier(jnp.mean(values * values, axis=-1, keepdims=True)) + EPS)
    return values * factor * gain

def slot_target(routing, capacity):
    listed = routing.reshape(-1)
    onehot = (listed[:, None] == jnp.arange(EXPERTS, dtype=jnp.int32)[None, :]).astype(jnp.int32)
    earlier = jnp.cumsum(onehot, axis=0) - onehot
    position = lax.optimization_barrier(jnp.sum(earlier * onehot, axis=1))
    return listed * capacity + position

def attention_branch(normed, w_query, w_key, w_value, w_out, segment_ids):
    length = normed.shape[0]
    group_size = HEADS // KV_HEADS
    score_scale = HEAD_DIM ** (-0.5)
    queries = low(low_back(matmul(normed, w_query))).reshape(length, KV_HEADS, group_size, HEAD_DIM)
    keys_all = low(low_back(matmul(normed, w_key))).reshape(length, KV_HEADS, HEAD_DIM)
    values_all = low(low_back(matmul(normed, w_value))).reshape(length, KV_HEADS, HEAD_DIM)
    scores = low_back(jnp.einsum('qhgd,khd->hgqk', queries, keys_all, precision=HIGH) * score_scale)
    places = jnp.arange(length, dtype=jnp.int32)
    allowed = (segment_ids[:, None] == segment_ids[None, :]) & (places[None, :] <= places[:, None])
    scores = jnp.where(allowed, scores, NEG)
    highest = lax.optimization_barrier(jnp.max(scores, axis=-1, keepdims=True))
    raised = jnp.exp(scores - highest)
    probs_low = low(raised / lax.optimization_barrier(jnp.sum(raised, axis=-1, keepdims=True)))
    mixture = jnp.einsum('hgqk,khd->qhgd', probs_low, values_all, precision=HIGH)
    mixture = low(low_back(mixture.reshape(length, HEADS * HEAD_DIM)))
    return low_back(matmul(mixture, w_out))

def expert_branch(normed, w_router, w_gate, w_up, w_down, routing):
    token_count = normed.shape[0]
    capacity = token_count // TOK_DEV * CAP
    logits = matmul(normed, w_router)
    choose = (routing[:, :, None] == jnp.arange(EXPERTS, dtype=jnp.int32)[None, None, :]).astype(jnp.float32)
    picked = lax.optimization_barrier(jnp.sum(choose * logits[:, None, :], axis=-1))
    gating = jax.nn.softmax(picked, axis=-1)
    target = slot_target(routing, capacity)
    spread = jnp.zeros((EXPERTS * capacity, D), jnp.float32).at[target].set(jnp.repeat(normed, TOP, axis=0))
    spread = spread.reshape(EXPERTS, capacity, D)
    gate_part = low_back(jnp.einsum('ecd,edf->ecf', spread, w_gate, precision=HIGH))
    up_part = low_back(jnp.einsum('ecd,edf->ecf', spread, w_up, precision=HIGH))
    hidden = low(jax.nn.silu(gate_part) * up_part)
    result = low_back(jnp.einsum('ecf,efd->ecd', hidden, w_down, precision=HIGH))
    chosen = result.reshape(EXPERTS * capacity, D)[target].reshape(token_count, TOP, D)
    return lax.optimization_barrier(jnp.sum(gating[:, :, None] * chosen, axis=1))

def block_forward(inputs, params, segment_ids, routing):
    norm_first, w_query, w_key, w_value, w_out, norm_second, w_router, w_gate, w_up, w_down = params
    normed_first = low(rms_norm(inputs, norm_first))
    middle = inputs + attention_branch(normed_first, w_query, w_key, w_value, w_out, segment_ids)
    normed_second = low(rms_norm(middle, norm_second))
    return middle + expert_branch(normed_second, w_router, w_gate, w_up, w_down, routing)

def reference(tokens, segments, routes, cotangent, norm1, w_query, w_key, w_value, w_out, norm2, w_router, w_gate, w_up, w_down):
    weights = tuple((weight.astype(jnp.float32) for weight in (norm1, w_query, w_key, w_value, w_out, norm2, w_router, w_gate, w_up, w_down)))
    seq_count = MICRO * SEQS
    sources = (tokens.reshape(seq_count, LEN, D), segments.reshape(seq_count, LEN), routes.reshape(seq_count, LEN, TOP), cotangent.reshape(seq_count, LEN, D))

    def advance(totals, pieces):
        inputs, segment_ids, routing, upstream = pieces

        def forward(values, params):
            return block_forward(values, params, segment_ids, routing)
        output, puller = jax.vjp(forward, inputs.astype(jnp.float32), weights)
        grad_inputs, grad_weights = puller(upstream.astype(jnp.float32))
        totals = tuple((former + latter for former, latter in zip(totals, grad_weights)))
        return (totals, (output.astype(jnp.bfloat16), grad_inputs))
    initial = tuple((jnp.zeros(weight.shape, jnp.float32) for weight in weights))
    totals, (outputs, grads_in) = lax.scan(advance, initial, sources)
    return (outputs.reshape(MICRO, SEQS, LEN, D), grads_in.reshape(MICRO, SEQS, LEN, D), totals[0], totals[1], totals[2], totals[3], totals[4], totals[5], totals[6], totals[7], totals[8], totals[9])
```

```python
import functools

import jax
import jax.numpy as jnp
from jax import lax
from jax.experimental import pallas as pl
from jax.experimental.pallas import tpu as pltpu
from jax.sharding import PartitionSpec as P

D = 1536
HEADS = 24
HEAD_DIM = 64
KV_HEADS = 8
EXPERTS = 4
MICRO = 2
GROUP = HEADS // KV_HEADS
SCALE = HEAD_DIM**-0.5
EPS = 1e-05
NEG = -1e30
BF = jnp.bfloat16
F32 = jnp.float32


class Ring:
    def __init__(self, n):
        self.n = n
        self.order = list(range(0, n, 2)) + list(range(n - 1, 0, -2))
        self.up = [(self.order[i], self.order[(i + 1) % n]) for i in range(n)]
        self.down = [(b, a) for a, b in self.up]
        index = lax.axis_index("fsdp")
        self.place = jnp.where(index % 2 == 0, index // 2, n - 1 - index // 2)

    def owner(self, offset):
        place = (self.place + offset) % self.n
        return jnp.where(place < self.n // 2, 2 * place, 2 * (self.n - 1 - place) + 1)

    def reach(self, flip):
        far = self.n // 2
        near = self.n - 1 - far
        return (near, far) if flip else (far, near)

    def gather(self, chunk, flip):
        ahead, behind = self.reach(flip)
        got = [(0, chunk)]
        one, two = chunk, chunk
        for step in range(1, max(ahead, behind) + 1):
            if step <= ahead:
                one = lax.ppermute(one, "fsdp", self.up)
                got.append((-step, one))
            if step <= behind:
                two = lax.ppermute(two, "fsdp", self.down)
                got.append((step, two))
        return got

    def join(self, got):
        rows, columns = got[0][1].shape
        whole = jnp.zeros((self.n, rows, columns), got[0][1].dtype)
        for offset, chunk in got:
            whole = lax.dynamic_update_slice(whole, chunk[None], (self.owner(offset), 0, 0))
        return whole.reshape(self.n * rows, columns)

    def scatter(self, terms, flip):
        ahead, behind = self.reach(flip)

        def own(offset):
            return lax.dynamic_index_in_dim(terms, self.owner(offset), 0, keepdims=False)

        one, two = own(ahead).astype(BF), own(-behind).astype(BF)
        for step in range(1, max(ahead, behind) + 1):
            if step <= ahead:
                one = lax.ppermute(one, "fsdp", self.up)
                if step < ahead:
                    one = (one.astype(F32) + own(ahead - step).astype(F32)).astype(BF)
            if step <= behind:
                two = lax.ppermute(two, "fsdp", self.down)
                if step < behind:
                    two = (two.astype(F32) + own(step - behind).astype(F32)).astype(BF)
        return own(0).astype(F32) + one.astype(F32) + two.astype(F32)


CORE = [(i, i ^ 1) for i in range(4)]
FAR = [(i, i ^ 2) for i in range(4)]


def seq_gather(block):
    first = lax.ppermute(block, "seq", CORE)
    second = lax.ppermute(block, "seq", FAR)
    third = lax.ppermute(second, "seq", CORE)
    return jnp.stack([block, first, second, third])


def seq_scatter(terms):
    third = lax.ppermute(terms[3].astype(BF), "seq", CORE)
    send = (terms[2].astype(F32) + third.astype(F32)).astype(BF)
    second = lax.ppermute(send, "seq", FAR)
    first = lax.ppermute(terms[1].astype(BF), "seq", CORE)
    return terms[0].astype(F32) + first.astype(F32) + second.astype(F32)


def mm(a, b, dims=((1,), (0,))):
    return lax.dot_general(a, b, (dims, ((), ())), preferred_element_type=F32)


def attend_kernel(heads, qkv_ref, bias_ref, o_ref):
    length = bias_ref.shape[1]
    qkv = qkv_ref[:, 0].reshape(length, qkv_ref.shape[-1])
    bias = bias_ref[0]
    groups = heads // GROUP
    mixed = []
    for kv in range(groups):
        key = qkv[:, (heads + kv) * HEAD_DIM : (heads + kv + 1) * HEAD_DIM]
        value = qkv[:, (heads + groups + kv) * HEAD_DIM : (heads + groups + kv + 1) * HEAD_DIM]
        for head in range(kv * GROUP, (kv + 1) * GROUP):
            query = qkv[:, head * HEAD_DIM : (head + 1) * HEAD_DIM]
            scores = mm(query, key, ((1,), (1,))) * SCALE + bias
            raised = jnp.exp(scores - jnp.max(scores, axis=-1, keepdims=True))
            probs = raised / jnp.sum(raised, axis=-1, keepdims=True)
            mixed.append(mm(probs.astype(BF), value).astype(BF))
    o_ref[:, 0] = jnp.concatenate(mixed, axis=1).reshape(o_ref.shape[0], *o_ref.shape[2:])


def attend_back_kernel(heads, qkv_ref, do_ref, bias_ref, d_ref):
    length = bias_ref.shape[1]
    qkv = qkv_ref[:, 0].reshape(length, qkv_ref.shape[-1])
    grad = do_ref[:, 0].reshape(length, do_ref.shape[-1])
    bias = bias_ref[0]
    groups = heads // GROUP
    grad_query, grad_key, grad_value = [], [], []
    for kv in range(groups):
        key = qkv[:, (heads + kv) * HEAD_DIM : (heads + kv + 1) * HEAD_DIM]
        value = qkv[:, (heads + groups + kv) * HEAD_DIM : (heads + groups + kv + 1) * HEAD_DIM]
        sum_key = jnp.zeros((length, HEAD_DIM), F32)
        sum_value = jnp.zeros((length, HEAD_DIM), F32)
        for head in range(kv * GROUP, (kv + 1) * GROUP):
            query = qkv[:, head * HEAD_DIM : (head + 1) * HEAD_DIM]
            upstream = grad[:, head * HEAD_DIM : (head + 1) * HEAD_DIM]
            scores = mm(query, key, ((1,), (1,))) * SCALE + bias
            raised = jnp.exp(scores - jnp.max(scores, axis=-1, keepdims=True))
            probs = raised / jnp.sum(raised, axis=-1, keepdims=True)
            dp = mm(upstream, value, ((1,), (1,)))
            ds = (probs * (dp - jnp.sum(dp * probs, axis=-1, keepdims=True))).astype(BF)
            grad_query.append((mm(ds, key) * SCALE).astype(BF))
            sum_key += mm(ds, query, ((0,), (0,)))
            sum_value += mm(probs.astype(BF), upstream, ((0,), (0,)))
        grad_key.append((sum_key * SCALE).astype(BF))
        grad_value.append(sum_value.astype(BF))
    whole = jnp.concatenate(grad_query + grad_key + grad_value, axis=1)
    d_ref[:, 0] = whole.reshape(d_ref.shape[0], *d_ref.shape[2:])


def attention(kernel, outs, bias, *arrays):
    blocks, micro, rows, _ = arrays[0].shape

    def spec(columns):
        return pl.BlockSpec((blocks, 1, rows, columns), lambda m: (0, m, 0, 0))

    length = bias.shape[1]
    return pl.pallas_call(
        kernel,
        grid=(micro,),
        in_specs=[spec(a.shape[-1]) for a in arrays]
        + [pl.BlockSpec((1, length, length), lambda m: (m, 0, 0))],
        out_specs=spec(outs),
        out_shape=jax.ShapeDtypeStruct((blocks, micro, rows, outs), BF),
        cost_estimate=pl.CostEstimate(flops=4 * 10**8, bytes_accessed=4 * 10**6, transcendentals=10**6),
    )(*arrays, bias)


def on_device(
    tokens, segments, routes, cotangent, norm1, w_query, w_key, w_value, w_out,
    norm2, w_router, w_gate, w_up, w_down,
):
    seq = lax.axis_index("seq")
    parts = lax.axis_size("seq")
    ring = Ring(lax.axis_size("fsdp"))
    micro, rows = tokens.shape[0], tokens.shape[2]
    own = micro * rows
    count = parts * own
    chunk = w_query.shape[0]
    q_cols, kv_cols = w_query.shape[1], w_key.shape[1]
    qkv_cols = q_cols + 2 * kv_cols
    heads = q_cols // HEAD_DIM
    hidden = w_gate.shape[2]
    wide = EXPERTS * hidden

    def flat(w):
        return jnp.swapaxes(w, 0, 1).reshape(w.shape[1], -1)

    def unflat(g):
        return jnp.swapaxes(g.reshape(g.shape[0], EXPERTS, -1), 0, 1)

    small = jnp.concatenate([norm1[None], norm2[None], w_router.T], axis=0)
    small = lax.all_gather(small, "fsdp", axis=1, tiled=True).astype(F32)
    gain_one, gain_two, router = small[0], small[1], small[2:]

    attn_w = ring.join(ring.gather(jnp.concatenate([w_query, w_key, w_value, w_out.T], axis=1), False))
    gate_w = ring.join(ring.gather(flat(w_gate), True))
    up_w = ring.join(ring.gather(flat(w_up), False))
    down_w = ring.join(ring.gather(flat(jnp.swapaxes(w_down, 1, 2)), True))
    qkv_w, out_w = attn_w[:, :qkv_cols], attn_w[:, qkv_cols:]

    x_own = tokens.reshape(own, D)
    x_all = seq_gather(x_own).reshape(count, D)
    dy_own = cotangent.reshape(own, D)
    dy_all = seq_gather(dy_own).reshape(count, D)

    block_ids = seq ^ jnp.arange(parts, dtype=jnp.int32)
    places = (block_ids[:, None] * rows + jnp.arange(rows, dtype=jnp.int32)[None]).reshape(-1)
    seg = jnp.take(segments[:, 0].reshape(micro, parts, rows), block_ids, axis=1).reshape(micro, -1)
    allowed = (seg[:, :, None] == seg[:, None, :]) & (places[None, None, :] <= places[None, :, None])
    bias = jnp.where(allowed, 0.0, NEG).astype(F32)
    route = jnp.take(routes[:, 0].reshape(micro, parts, rows, 2), block_ids, axis=1)
    route = jnp.swapaxes(route, 0, 1).reshape(count, 2)
    ids = jnp.arange(EXPERTS, dtype=jnp.int32)
    chosen = (route[:, :1] == ids) | (route[:, 1:] == ids)

    def norm(v, gain):
        factor = lax.rsqrt(jnp.mean(v * v, axis=-1, keepdims=True) + EPS)
        return v * factor, (v * factor * gain).astype(BF), factor

    def norm_back(normal, factor, gain, upstream):
        scaled = upstream * gain
        grad_gain = jnp.sum(upstream * normal, axis=0)
        return factor * (scaled - normal * jnp.mean(scaled * normal, axis=-1, keepdims=True)), grad_gain

    _, n1, _ = norm(x_all.astype(F32), gain_one)
    qkv = mm(n1, qkv_w).astype(BF)
    shape4 = (parts, micro, rows, -1)
    mixed = attention(functools.partial(attend_kernel, heads), q_cols, bias, qkv.reshape(shape4))
    mixed = mixed.reshape(count, q_cols)
    part = mm(mixed, out_w, ((1,), (1,)))
    h = x_own.astype(F32) + seq_scatter(part.reshape(parts, own, D))

    c2, n2_own, r2 = norm(h, gain_two)
    n2 = seq_gather(n2_own).reshape(count, D)
    logits = mm(n2, router.astype(BF), ((1,), (1,)))
    masked = jnp.where(chosen, logits, NEG)
    raised = jnp.where(chosen, jnp.exp(masked - jnp.max(masked, axis=-1, keepdims=True)), 0.0)
    gating = raised / jnp.sum(raised, axis=-1, keepdims=True)

    def each(v):
        return jnp.broadcast_to(v[:, :, None], (count, EXPERTS, hidden)).reshape(count, wide)

    g = mm(n2, gate_w)
    u = mm(n2, up_w)
    sig = jax.nn.sigmoid(g)
    act = g * sig
    z = act * u
    weight = each(gating)
    zg = (z * weight).astype(BF)
    grad_down = mm(dy_all, zg, ((0,), (0,))).astype(BF)
    dz = mm(dy_all, down_w)
    dgate = jnp.sum((z * dz).reshape(count, EXPERTS, hidden), axis=-1)
    dlogits = gating * (dgate - jnp.sum(gating * dgate, axis=-1, keepdims=True))
    dz = dz * weight
    dg = (dz * u * sig * (1.0 + g * (1.0 - sig))).astype(BF)
    du = (dz * act).astype(BF)
    dn2 = mm(dg, gate_w, ((1,), (1,))) + mm(du, up_w, ((1,), (1,)))
    dn2 = dn2 + lax.dot_general(
        dlogits, router, (((1,), (0,)), ((), ())), precision=lax.Precision.HIGHEST
    )
    y_part = mm(zg, down_w, ((1,), (1,)))
    grad_gate = mm(n2, dg, ((0,), (0,))).astype(BF)
    grad_up = mm(n2, du, ((0,), (0,))).astype(BF)
    grad_router = lax.dot_general(
        dlogits, n2.astype(F32), (((0,), (0,)), ((), ())), precision=lax.Precision.HIGHEST
    )

    def owners(grad):
        return grad.reshape(ring.n, chunk, -1)

    sum_down = ring.scatter(owners(grad_down), False)
    sum_gate = ring.scatter(owners(grad_gate), True)
    sum_up = ring.scatter(owners(grad_up), False)
    layer_out = (h + seq_scatter(y_part.reshape(parts, own, D))).astype(BF)
    dn2_own = seq_scatter(dn2.reshape(parts, own, D))
    dh_norm, grad_norm2 = norm_back(c2, r2, gain_two, dn2_own)
    dh = dy_own.astype(F32) + dh_norm

    da = seq_gather(dh.astype(BF)).reshape(count, D)
    grad_out = mm(da, mixed, ((0,), (0,))).astype(BF)
    do = mm(da, out_w).astype(BF)
    dqkv = attention(
        functools.partial(attend_back_kernel, heads), qkv_cols, bias, qkv.reshape(shape4), do.reshape(shape4)
    ).reshape(count, qkv_cols)
    grad_qkv = mm(n1, dqkv, ((0,), (0,))).astype(BF)
    dn1 = mm(dqkv, qkv_w, ((1,), (1,)))
    sum_out = ring.scatter(owners(grad_out), True)
    sum_qkv = ring.scatter(owners(grad_qkv), False)
    dn1_own = seq_scatter(dn1.reshape(parts, own, D))
    c1, _, r1 = norm(x_own.astype(F32), gain_one)
    dx, grad_norm1 = norm_back(c1, r1, gain_one, dn1_own)
    grad_input = dh + dx

    tiny = jnp.concatenate([grad_norm1[None], grad_norm2[None], grad_router], axis=0)
    tiny = lax.psum(tiny, ("seq", "fsdp"))
    tiny = lax.dynamic_slice_in_dim(tiny, lax.axis_index("fsdp") * chunk, chunk, axis=1)

    lead = (micro, 1, rows, D)
    return (
        layer_out.reshape(lead),
        grad_input.reshape(lead),
        tiny[0],
        sum_qkv[:, :q_cols],
        sum_qkv[:, q_cols : q_cols + kv_cols],
        sum_qkv[:, q_cols + kv_cols :],
        sum_out.T,
        tiny[1],
        tiny[2:].T,
        unflat(sum_gate),
        unflat(sum_up),
        jnp.swapaxes(unflat(sum_down), 1, 2),
    )


def solution(mesh):
    return jax.shard_map(
        on_device,
        mesh=mesh,
        in_specs=(
            P(None, "fsdp", "seq", None),
            P(None, "fsdp", None),
            P(None, "fsdp", None, None),
            P(None, "fsdp", "seq", None),
            P("fsdp"),
            P("fsdp", "seq"),
            P("fsdp", "seq"),
            P("fsdp", "seq"),
            P("seq", "fsdp"),
            P("fsdp"),
            P("fsdp", None),
            P(None, "fsdp", "seq"),
            P(None, "fsdp", "seq"),
            P(None, "seq", "fsdp"),
        ),
        out_specs=(
            P(None, "fsdp", "seq", None),
            P(None, "fsdp", "seq", None),
            P("fsdp"),
            P("fsdp", "seq"),
            P("fsdp", "seq"),
            P("fsdp", "seq"),
            P("seq", "fsdp"),
            P("fsdp"),
            P("fsdp", None),
            P(None, "fsdp", "seq"),
            P(None, "fsdp", "seq"),
            P(None, "seq", "fsdp"),
        ),
        check_vma=False,
    )
```

```python
import functools

import jax
import jax.numpy as jnp
from jax import lax
from jax.experimental import pallas as pl
from jax.experimental.pallas import tpu as pltpu
from jax.sharding import PartitionSpec as P


D = 1536
HEADS = 24
HEAD_DIM = 64
KV_HEADS = 8
EXPERTS = 4
GROUP = HEADS // KV_HEADS
SCALE = HEAD_DIM**-0.5
EPS = 1e-05
NEG = -1e30
BF = jnp.bfloat16
F32 = jnp.float32
LANES = 128
EXTRA = 16
PAIR = 2
TILE = 384

VMEM = pl.BlockSpec(memory_space=pltpu.VMEM)
SMEM = pl.BlockSpec(memory_space=pltpu.SMEM)
ANY = pl.BlockSpec(memory_space=pl.ANY)


def mm(a, b, dims=((1,), (0,))):
    return lax.dot_general(a, b, (dims, ((), ())), preferred_element_type=F32)


def move(value, axis, bit):
    return lax.ppermute(value, axis, [(i, i ^ bit) for i in range(lax.axis_size(axis))])


def move_both(value, seq_bit, fsdp_bit):
    n = lax.axis_size("fsdp")
    pairs = [
        (s * n + f, (s ^ seq_bit) * n + (f ^ fsdp_bit))
        for s in range(lax.axis_size("seq"))
        for f in range(n)
    ]
    return lax.ppermute(value, ("seq", "fsdp"), pairs)


def spread(mine, other, n):
    units = [None] * n
    units[0] = mine
    for d in sorted(range(2, n, 2), key=lambda d: (d & (d - 1) != 0, -d)):
        units[d] = move(other if d & PAIR else mine, "fsdp", d)
    for d in range(0, n, 2):
        units[d ^ 1] = move(units[d], "fsdp", 1)
    return units


def collect(even, odd, n):
    odd = move(odd, "fsdp", 1)
    sums = [even[i].astype(F32) + odd[i].astype(F32) for i in range(n // 2)]
    got = {0: sums[0]}
    for i in range(n // 2 - 1, 0, -1):
        got[2 * i] = move(sums[i].astype(BF), "fsdp", 2 * i)
    return got


def total(parts):
    out = parts[0].astype(F32)
    for part in parts[1:]:
        out = out + part.astype(F32)
    return out


def add(a, b):
    return (a.astype(F32) + b.astype(F32)).astype(BF)


def seq_gather(block):
    second = move(block, "seq", 2)
    first = move(block, "seq", 1)
    third = move(second, "seq", 1)
    return [block, first, second, third]


def seq_scatter(terms):
    third = move(terms[3], "seq", 1)
    second = move(add(terms[2], third), "seq", 2)
    first = move(terms[1], "seq", 1)
    return [terms[0], first, second]


BLOCKS = ((0, 0), (2, 0), (0, PAIR), (2, PAIR), (1, 0), (3, 0), (1, PAIR), (3, PAIR))


def wide_gather(block):
    pair = move(block, "fsdp", PAIR)
    far = move(block, "seq", 2)
    both = move(pair, "seq", 2)
    near = [block, far, pair, both]
    return near + [move(b, "seq", 1) for b in near]


def wide_scatter(near, away):
    away = move(away, "seq", 1)
    both = move_both(add(near[3], away[3]), 2, PAIR)
    pair = move(add(near[2], away[2]), "fsdp", PAIR)
    far = move(add(near[1], away[1]), "seq", 2)
    return [near, away, far, pair, both]


def call(kernel, outs, scratch, specs, args, flops, moved, out_specs=None, grid=()):
    return pl.pallas_call(
        kernel,
        grid=grid,
        in_specs=specs,
        out_specs=out_specs or [VMEM] * len(outs),
        out_shape=[jax.ShapeDtypeStruct(s, d) for s, d in outs],
        scratch_shapes=scratch,
        compiler_params=pltpu.CompilerParams(vmem_limit_bytes=56 * 2**20),
        cost_estimate=pl.CostEstimate(
            flops=int(flops), bytes_accessed=int(moved), transcendentals=0
        ),
    )(*args)


def normal(v):
    return v * lax.rsqrt(jnp.mean(v * v, axis=-1, keepdims=True) + EPS)


def rows_of(owners, k, rows):
    return pl.ds(pl.multiple_of(owners[k] * rows, 16), rows)


def slabs(ref, micro, rows):
    per = ref.shape[0] // 4
    return jnp.concatenate([ref[pl.ds(j * per + micro * rows, rows)] for j in range(4)], axis=0)


def softmax(query, key, bias):
    scores = mm(query, key, ((1,), (1,))) + bias
    raised = jnp.exp(scores - jnp.max(scores, axis=-1, keepdims=True))
    return raised * (1.0 / jnp.sum(raised, axis=-1, keepdims=True))


def attn_pack_kernel(q_ref, k_ref, v_ref, o_ref, one_ref, two_ref, router_ref, out_ref):
    chunk, at = q_ref.shape[0], 0
    for ref in (q_ref, k_ref, v_ref, o_ref):
        out_ref[:chunk, at : at + ref.shape[1]] = ref[...]
        at += ref.shape[1]
    rest = jnp.zeros((EXTRA - 2 - EXPERTS, chunk), F32)
    small = [one_ref[...].reshape(1, chunk), two_ref[...].reshape(1, chunk), router_ref[...]]
    out_ref[chunk:, :chunk] = jnp.concatenate([v.astype(F32) for v in small] + [rest], axis=0).astype(BF)


def expert_pack_kernel(side, gate_ref, up_ref, down_ref, mine_ref, other_ref):
    hidden = gate_ref.shape[2] // 2
    wide = EXPERTS * hidden
    for e in range(EXPERTS):
        down = down_ref[e]
        for half in range(2):
            at = slice(half * hidden, (half + 1) * hidden)
            to = slice(e * hidden, (e + 1) * hidden)

            def put(ref):
                ref[:, to] = gate_ref[e, :, at]
                ref[:, slice(wide + to.start, wide + to.stop)] = up_ref[e, :, at]
                ref[:, slice(2 * wide + to.start, 2 * wide + to.stop)] = down[:, at]

            pl.when(side[0] == half)(functools.partial(put, mine_ref))
            pl.when(side[0] != half)(functools.partial(put, other_ref))


def norm_kernel(x_ref, a_ref, b_ref, c_ref, gain_ref, h_ref, n_ref):
    h = total([x_ref[...], a_ref[...], b_ref[...], c_ref[...]])
    h_ref[...] = h
    n_ref[...] = (normal(h) * gain_ref[1:2]).astype(BF)


def norm_back(v, gain, upstream):
    factor = lax.rsqrt(jnp.mean(v * v, axis=-1, keepdims=True) + EPS)
    normed = v * factor
    scaled = upstream * gain
    back = factor * (scaled - normed * jnp.mean(scaled * normed, axis=-1, keepdims=True))
    return back, jnp.sum(upstream * normed, axis=0, keepdims=True)


def norm_back_kernel(near_ref, away_ref, a_ref, b_ref, c_ref, h_ref, dy_ref, gain_ref, dh_ref, da_ref, g_ref):
    dn2 = total([near_ref[0], away_ref[0], a_ref[...], b_ref[...], c_ref[...]])
    back, grad = norm_back(h_ref[...], gain_ref[1:2], dn2)
    dh = dy_ref[...].astype(F32) + back
    dh_ref[...] = dh
    da_ref[...] = dh.astype(BF)
    g_ref[...] = grad


def input_kernel(x_ref, a_ref, b_ref, c_ref, dh_ref, gain_ref, out_ref):
    dn1 = total([a_ref[...], b_ref[...], c_ref[...]])
    out_ref[...] = dh_ref[...] + norm_back(x_ref[...].astype(F32), gain_ref[0:1], dn1)[0]


def attend_kernel(n, heads, owners, *refs):
    x_refs, pieces, refs = refs[:4], refs[4 : 4 + n], refs[4 + n :]
    bias_ref, n1_ref, qkv_ref, mix_ref, small_ref, *refs = refs
    part_refs, (w, extra, sem) = refs[:4], refs[4:]
    chunk = D // n
    copies = []
    for k, piece in enumerate(pieces):
        copies.append(
            pltpu.make_async_copy(piece.at[:chunk], w.at[rows_of(owners, k, chunk)], sem.at[0, k])
        )
        copies.append(
            pltpu.make_async_copy(
                piece.at[chunk:, : extra.shape[2]], extra.at[owners[k]], sem.at[1, k]
            )
        )
    for copy in copies:
        copy.start()
    block = x_refs[0].shape[0]
    q_cols = heads * HEAD_DIM
    kv_cols = q_cols // GROUP
    qkv_cols = q_cols + 2 * kv_cols
    for copy in copies:
        copy.wait()
    small = jnp.concatenate([extra[j].astype(F32)[:, :chunk] for j in range(n)], axis=1)
    small_ref[...] = small
    gain = small[0:1]
    for j in range(4):
        n1_ref[j * block : (j + 1) * block] = (normal(x_refs[j][...].astype(F32)) * gain).astype(BF)
    qkv_ref[...] = mm(n1_ref[...], w[:, :qkv_cols]).astype(BF)
    micro, rows = bias_ref.shape[0], bias_ref.shape[1] // 4
    for m in range(micro):
        qkv = slabs(qkv_ref, m, rows)
        bias = bias_ref[m]
        mixed = []
        for head in range(heads):
            kv = head // GROUP
            key = qkv[:, q_cols + kv * HEAD_DIM : q_cols + (kv + 1) * HEAD_DIM]
            value = qkv[:, q_cols + kv_cols + kv * HEAD_DIM : q_cols + kv_cols + (kv + 1) * HEAD_DIM]
            query = qkv[:, head * HEAD_DIM : (head + 1) * HEAD_DIM] * BF(SCALE)
            mixed.append(mm(softmax(query, key, bias).astype(BF), value).astype(BF))
        mixed = jnp.concatenate(mixed, axis=1)
        for j in range(4):
            mix_ref[pl.ds(j * block + m * rows, rows)] = mixed[j * rows : (j + 1) * rows]
    for j in range(4):
        mixed = mix_ref[j * block : (j + 1) * block]
        part_refs[j][...] = mm(mixed, w[:, qkv_cols:], ((1,), (1,))).astype(BF)


def store_units(even_ref, odd_ref, mine, first, value):
    rows = even_ref.shape[1]
    flag = (mine & 1) == 1
    for i in range(value.shape[0] // (2 * rows)):
        a = value[2 * i * rows : (2 * i + 1) * rows]
        b = value[(2 * i + 1) * rows : (2 * i + 2) * rows]
        slot = (mine >> 1) ^ (first + i)
        even_ref[slot] = jnp.where(flag, b, a).astype(BF)
        odd_ref[slot] = jnp.where(flag, a, b).astype(BF)


def tiles(rows, body):
    per = TILE // (2 * rows)

    def step(i, carry):
        body(pl.ds(pl.multiple_of(i * TILE, TILE), TILE), i * per)
        return carry

    lax.fori_loop(0, D // TILE, step, 0)


def out_back_kernel(n, owners, mine, *refs):
    da_refs, pieces, refs = refs[:4], refs[4 : 4 + n], refs[4 + n :]
    mix_ref, do_ref, even_ref, odd_ref, w, da_all, sem = refs
    chunk, q_cols = D // n, mix_ref.shape[1]
    copies = [
        pltpu.make_async_copy(
            piece.at[:chunk, piece.shape[1] - q_cols :], w.at[rows_of(owners, k, chunk)], sem.at[k]
        )
        for k, piece in enumerate(pieces)
    ]
    for copy in copies:
        copy.start()
    block = da_refs[0].shape[0]
    for j in range(4):
        da_all[j * block : (j + 1) * block] = da_refs[j][...]

    def grads(at, first):
        store_units(even_ref, odd_ref, mine[0], first, mm(da_all[:, at], mix_ref[...], ((0,), (0,))))

    tiles(chunk, grads)
    for copy in copies:
        copy.wait()
    do_ref[...] = mm(da_all[...], w[...]).astype(BF)


def attend_back_kernel(n, heads, owners, mine, *refs):
    pieces, refs = refs[:n], refs[n:]
    n1_ref, qkv_ref, do_ref, bias_ref, d_ref, *unit_refs, gain_ref, w, sem = refs
    chunk, cols = D // n, w.shape[1]
    copies = [
        pltpu.make_async_copy(piece.at[:chunk, :cols], w.at[rows_of(owners, k, chunk)], sem.at[k])
        for k, piece in enumerate(pieces)
    ]
    for copy in copies:
        copy.start()
    q_cols = heads * HEAD_DIM
    kv_cols = q_cols // GROUP
    micro, rows = bias_ref.shape[0], bias_ref.shape[1] // 4
    block, length = n1_ref.shape[0] // 4, 4 * rows
    for m in range(micro):
        qkv = slabs(qkv_ref, m, rows)
        grad = slabs(do_ref, m, rows)
        bias = bias_ref[m]
        grad_query, grad_key, grad_value = [], [], []
        for kv in range(heads // GROUP):
            key = qkv[:, q_cols + kv * HEAD_DIM : q_cols + (kv + 1) * HEAD_DIM]
            value = qkv[:, q_cols + kv_cols + kv * HEAD_DIM : q_cols + kv_cols + (kv + 1) * HEAD_DIM]
            scaled = key * BF(SCALE)
            sum_key = jnp.zeros((length, HEAD_DIM), F32)
            sum_value = jnp.zeros((length, HEAD_DIM), F32)
            for head in range(kv * GROUP, (kv + 1) * GROUP):
                query = qkv[:, head * HEAD_DIM : (head + 1) * HEAD_DIM] * BF(SCALE)
                upstream = grad[:, head * HEAD_DIM : (head + 1) * HEAD_DIM]
                probs = softmax(query, key, bias)
                dp = mm(upstream, value, ((1,), (1,)))
                ds = (probs * (dp - jnp.sum(dp * probs, axis=-1, keepdims=True))).astype(BF)
                grad_query.append(mm(ds, scaled).astype(BF))
                sum_key += mm(ds, query, ((0,), (0,)))
                sum_value += mm(probs.astype(BF), upstream, ((0,), (0,)))
            grad_key.append(sum_key.astype(BF))
            grad_value.append(sum_value.astype(BF))
        whole = jnp.concatenate(grad_query + grad_key + grad_value, axis=1)
        for j in range(4):
            d_ref[pl.ds(j * block + m * rows, rows)] = whole[j * rows : (j + 1) * rows]

    for copy in copies:
        copy.wait()
    ones = jnp.ones((8, 2 * cols), BF)

    def grads(at, first):
        value = mm(n1_ref[:, at], d_ref[...], ((0,), (0,)))
        store_units(*unit_refs[:2], mine[0], first, value[:, :q_cols])
        store_units(*unit_refs[2:], mine[0], first, value[:, q_cols:])
        gain_ref[:, at] = mm(ones, split(value * w[at].astype(F32)), ((1,), (1,)))

    tiles(chunk, grads)


def input_grad_kernel(n, owners, *refs):
    pieces, refs = refs[:n], refs[n:]
    d_ref, *refs = refs
    part_refs, (w, sem) = refs[:4], refs[4:]
    chunk, cols = D // n, d_ref.shape[1]
    copies = [
        pltpu.make_async_copy(piece.at[:chunk, :cols], w.at[rows_of(owners, k, chunk)], sem.at[k])
        for k, piece in enumerate(pieces)
    ]
    for copy in copies:
        copy.start()
    for copy in copies:
        copy.wait()
    block = part_refs[0].shape[0]
    for j in range(4):
        part_refs[j][...] = mm(d_ref[j * block : (j + 1) * block], w[...], ((1,), (1,))).astype(BF)


def split(v):
    high = v.astype(BF)
    return jnp.concatenate([high, (v - high.astype(F32)).astype(BF)], axis=1)


ROWS = 256


def expert_kernel(n, owners, *refs):
    n2_refs, dy_refs, pieces, refs = refs[:8], refs[8:16], refs[16 : 16 + n], refs[16 + n :]
    router_ref, chosen_ref, zg_out, dgu_out, near_out, away_out, *refs = refs
    w, n2_all, dy_all, chosen_all, zg, dgu, part, wsem, tsem, csem, osem = refs
    count, wide = zg.shape
    block = n2_refs[0].shape[0]
    chunk = D // n
    per = ROWS // block
    steps = count // ROWS
    cut = 2 * wide + LANES

    def tile(i):
        return pl.ds(pl.multiple_of(i * ROWS, ROWS), ROWS)

    first = [pltpu.make_async_copy(router_ref, w.at[:, 2 * wide : cut], csem.at[0])]
    second = []
    for k, piece in enumerate(pieces):
        at = rows_of(owners, k, chunk)
        first.append(pltpu.make_async_copy(piece.at[:, : 2 * wide], w.at[at, : 2 * wide], wsem.at[0, k]))
        second.append(pltpu.make_async_copy(piece.at[:, 2 * wide :], w.at[at, cut:], wsem.at[1, k]))
    tokens = []
    for k in range(len(n2_refs)):
        at = pl.ds(k * block, block)
        tokens.append(pltpu.make_async_copy(n2_refs[k], n2_all.at[at], tsem.at[0, k]))
        tokens.append(pltpu.make_async_copy(dy_refs[k], dy_all.at[at], tsem.at[1, k]))
    tokens.append(pltpu.make_async_copy(chosen_ref, chosen_all, csem.at[1]))
    for copy in first + tokens[: 2 * per] + tokens[-1:] + second:
        copy.start()
    for copy in first + tokens[-1:] + second:
        copy.wait()
    for copy in tokens[2 * per : -1]:
        copy.start()
    lane = lax.broadcasted_iota(jnp.int32, (LANES, wide), 0)
    column = lax.broadcasted_iota(jnp.int32, (LANES, wide), 1)
    expand = (lane == column // (wide // EXPERTS)).astype(BF)
    expand_two = jnp.concatenate([expand, expand], axis=0)

    def out_copies(i, h):
        b = pl.ds(i * per, per)
        here = near_out if h == 0 else away_out
        there = pl.ds(i * per - h * 4, per)
        return [
            pltpu.make_async_copy(zg.at[tile(i)], zg_out.at[tile(i)], osem.at[0, i]),
            pltpu.make_async_copy(dgu.at[tile(i)], dgu_out.at[tile(i)], osem.at[1, i]),
            pltpu.make_async_copy(part.at[b], here.at[there], osem.at[2, i]),
        ]

    for i in range(steps):
        at = tile(i)
        for copy in tokens[2 * per * i : 2 * per * (i + 1)]:
            copy.wait()
        chosen = chosen_all[at] > 0
        big = mm(n2_all[at], w[:, :cut])
        dz = mm(dy_all[at], w[:, cut:])
        g, u = big[:, :wide], big[:, wide : 2 * wide]
        logits = jnp.where(chosen, big[:, 2 * wide :], 0.0)
        other = jnp.sum(logits, axis=-1, keepdims=True) - logits
        gating = jnp.where(chosen, 1.0 / (1.0 + jnp.exp(other - logits)), 0.0)
        weight = mm(split(gating), expand_two)
        sig = 0.5 * jnp.tanh(0.5 * g) + 0.5
        act = g * sig
        z = act * u
        zg[at] = (z * weight).astype(BF)
        dgate = jnp.where(chosen, mm((z * dz).astype(BF), expand, ((1,), (1,))), 0.0)
        dz = dz * weight
        dgu[at, :wide] = (dz * u * (sig + act * (1.0 - sig))).astype(BF)
        dgu[at, wide : 2 * wide] = (dz * act).astype(BF)
        dlogits = gating * (dgate - jnp.sum(gating * dgate, axis=-1, keepdims=True))
        dgu[at, 2 * wide :] = dlogits.astype(BF)
        dn2 = mm(dgu[at], w[:, :cut], ((1,), (1,)))
        for b in range(per):
            part[i * per + b] = dn2[b * block : (b + 1) * block].astype(BF)
        for copy in out_copies(i, i * 2 // steps):
            copy.start()
    for i in range(steps):
        for copy in out_copies(i, i * 2 // steps):
            copy.wait()


def down_grad_kernel(n, mine, *refs):
    dy_refs, (zg_ref, even_ref, odd_ref, dy_all, sem) = refs[:8], refs[8:]
    block = dy_refs[0].shape[0]
    copies = [
        pltpu.make_async_copy(ref, dy_all.at[pl.ds(k * block, block)], sem.at[k])
        for k, ref in enumerate(dy_refs)
    ]
    for copy in copies:
        copy.start()
    for copy in copies:
        copy.wait()

    def grads(at, first):
        store_units(even_ref, odd_ref, mine[0], first, mm(dy_all[:, at], zg_ref[...], ((0,), (0,))))

    tiles(D // n, grads)


def gate_grad_kernel(n, mine, *refs):
    n2_refs, refs = refs[:8], refs[8:]
    dgu_ref, gate_even, gate_odd, up_even, up_odd, router_ref, n2_all, sem = refs
    block = n2_refs[0].shape[0]
    copies = [
        pltpu.make_async_copy(ref, n2_all.at[pl.ds(k * block, block)], sem.at[k])
        for k, ref in enumerate(n2_refs)
    ]
    for copy in copies:
        copy.start()
    for copy in copies:
        copy.wait()
    wide = gate_even.shape[2]

    def grads(at, first):
        value = mm(n2_all[:, at], dgu_ref[...], ((0,), (0,)))
        store_units(gate_even, gate_odd, mine[0], first, value[:, :wide])
        store_units(up_even, up_odd, mine[0], first, value[:, wide : 2 * wide])
        router_ref[:, at] = value[:, 2 * wide :].T[:8]

    tiles(D // n, grads)


def expert_out_kernel(n, owners, *refs):
    pieces, (zg_ref, near_ref, away_ref, w, sem) = refs[:n], refs[n:]
    wide = zg_ref.shape[1]
    chunk = D // n
    copies = [
        pltpu.make_async_copy(piece.at[:, 2 * wide :], w.at[rows_of(owners, k, chunk)], sem.at[k])
        for k, piece in enumerate(pieces)
    ]
    for copy in copies:
        copy.start()
    for copy in copies:
        copy.wait()
    block = near_ref.shape[1]
    for h, ref in enumerate((near_ref, away_ref)):
        value = mm(zg_ref[pl.ds(h * 4 * block, 4 * block)], w[...], ((1,), (1,)))
        ref[...] = value.astype(BF).reshape(4, block, D)


def on_device(
    tokens, segments, routes, cotangent, norm1, w_query, w_key, w_value, w_out,
    norm2, w_router, w_gate, w_up, w_down,
):
    seq = lax.axis_index("seq")
    mine = lax.axis_index("fsdp")
    n = lax.axis_size("fsdp")
    parts = lax.axis_size("seq")
    owners = (mine ^ jnp.arange(n, dtype=jnp.int32)).astype(jnp.int32)
    me = mine.reshape(1).astype(jnp.int32)
    side = jnp.where(mine & PAIR, 1, 0)
    micro, rows = tokens.shape[0], tokens.shape[2]
    own = micro * rows
    count = parts * own
    chunk = w_query.shape[0]
    q_cols, kv_cols = w_query.shape[1], w_key.shape[1]
    qkv_cols = q_cols + 2 * kv_cols
    heads = q_cols // HEAD_DIM
    hidden = w_gate.shape[2] // 2
    wide = EXPERTS * hidden

    (attn,) = call(
        attn_pack_kernel, [((chunk + EXTRA, qkv_cols + q_cols), BF)], [], [VMEM] * 7,
        [w_query, w_key, w_value, w_out.T, norm1, norm2, w_router.T], 0, 1e6,
    )
    attn_w = spread(attn, attn, n)
    x_own = tokens.reshape(own, D)
    dy_own = cotangent.reshape(own, D)
    x_all = seq_gather(x_own)

    here, there = call(
        expert_pack_kernel, [((chunk, 3 * wide), BF)] * 2, [], [SMEM] + [VMEM] * 3,
        [side.reshape(1).astype(jnp.int32), w_gate, w_up, jnp.swapaxes(w_down, 1, 2)], 0, 3e6,
    )
    expert_w = spread(here, there, n)
    dy_all = wide_gather(dy_own)

    ids = seq ^ jnp.arange(parts, dtype=jnp.int32)
    places = (ids[:, None] * rows + jnp.arange(rows, dtype=jnp.int32)[None]).reshape(-1)
    seg = jnp.take(segments[:, 0].reshape(micro, parts, rows), ids, axis=1).reshape(micro, -1)
    allowed = (seg[:, :, None] == seg[:, None, :]) & (places[None, None, :] <= places[None, :, None])
    bias = jnp.where(allowed, 0.0, NEG).astype(F32)
    here = routes[:, 0].reshape(-1, LANES)
    both = jnp.stack([here, move(here, "fsdp", PAIR)]).reshape(2, micro, parts, rows, 2)
    route = jnp.stack([both[1 if k else 0][:, seq ^ j] for j, k in BLOCKS]).reshape(-1, 2)
    lane = jnp.arange(LANES, dtype=jnp.int32)
    chosen = ((route[:, :1] == lane) | (route[:, 1:] == lane)).astype(F32)

    dma = pltpu.SemaphoreType.DMA
    block = ((own, D), BF)
    n1, qkv, mixed, small, *part = call(
        functools.partial(attend_kernel, n, heads),
        [((count, D), BF), ((count, qkv_cols), BF), ((count, q_cols), BF), ((EXTRA, D), F32)] + [block] * 4,
        [pltpu.VMEM((D, qkv_cols + q_cols), BF), pltpu.VMEM((n, EXTRA, 2 * LANES), BF), dma((2, n))],
        [SMEM] + [VMEM] * 4 + [ANY] * n + [VMEM],
        [owners, *x_all, *attn_w, bias],
        6e9, 9e6,
    )
    router = jnp.pad(small[2:6].astype(BF), ((0, LANES - 4), (0, 0))).T
    h, n2_own = call(
        norm_kernel, [((own, D), F32), block], [], [VMEM] * 5,
        [x_own, *seq_scatter(part), small], 0, 3e6,
    )
    n2_all = wide_gather(n2_own)
    span = len(BLOCKS) * own
    four = ((4, own, D), BF)
    zg, dgu, near, away = call(
        functools.partial(expert_kernel, n),
        [((span, wide), BF), ((span, 2 * wide + LANES), BF), four, four],
        [
            pltpu.VMEM((D, 3 * wide + LANES), BF), pltpu.VMEM((span, D), BF), pltpu.VMEM((span, D), BF),
            pltpu.VMEM((span, LANES), F32), pltpu.VMEM((span, wide), BF),
            pltpu.VMEM((span, 2 * wide + LANES), BF), pltpu.VMEM((len(BLOCKS), own, D), BF),
            dma((2, n)), dma((2, len(BLOCKS))), dma((2,)), dma((3, span // ROWS)),
        ],
        [SMEM] + [ANY] * (18 + n),
        [owners, *n2_all, *dy_all, *expert_w, router, chosen],
        8e9, 18e6, [ANY] * 4,
    )
    units = ((n // 2, chunk, wide), BF)
    down_even, down_odd = call(
        functools.partial(down_grad_kernel, n),
        [units] * 2,
        [pltpu.VMEM((span, D), BF), dma((len(BLOCKS),))],
        [SMEM] + [ANY] * 8 + [VMEM],
        [me, *dy_all, zg],
        1.6e9, 6e6,
    )
    dn2 = wide_scatter(near, away)
    gate_even, gate_odd, up_even, up_odd, grad_router = call(
        functools.partial(gate_grad_kernel, n),
        [units] * 4 + [((8, D), F32)],
        [pltpu.VMEM((span, D), BF), dma((len(BLOCKS),))],
        [SMEM] + [ANY] * 8 + [VMEM],
        [me, *n2_all, dgu],
        3.5e9, 9e6,
    )

    def share(got):
        near = total([got[d] for d in got if not d & PAIR])
        pair = total([got[d] for d in got if d & PAIR])
        low = jnp.where(side == 0, near, pair).reshape(chunk, EXPERTS, hidden)
        high = jnp.where(side == 0, pair, near).reshape(chunk, EXPERTS, hidden)
        return jnp.swapaxes(jnp.concatenate([low, high], axis=2), 0, 1)

    got_down = collect(down_even, down_odd, n)
    got_gate = collect(gate_even, gate_odd, n)
    got_up = collect(up_even, up_odd, n)

    corner = pl.BlockSpec((1, own, D), lambda i: (0, 0, 0))
    dh, da, grad_norm2 = call(
        norm_back_kernel, [((own, D), F32), block, ((1, D), F32)], [], [corner] * 2 + [VMEM] * 6,
        [*dn2, h, dy_own, small], 0, 5e6, grid=(1,),
    )

    da = seq_gather(da)
    y_near, y_away = call(
        functools.partial(expert_out_kernel, n),
        [four, four],
        [pltpu.VMEM((D, wide), BF), dma((n,))],
        [SMEM] + [ANY] * n + [VMEM],
        [owners, *expert_w, zg],
        1.6e9, 6e6,
    )
    do, out_even, out_odd = call(
        functools.partial(out_back_kernel, n),
        [((count, q_cols), BF), ((n // 2, chunk, q_cols), BF), ((n // 2, chunk, q_cols), BF)],
        [pltpu.VMEM((D, q_cols), BF), pltpu.VMEM((count, D), BF), dma((n,))],
        [SMEM] * 2 + [VMEM] * 4 + [ANY] * n + [VMEM],
        [owners, me, *da, *attn_w, mixed],
        1.2e9, 4e6,
    )
    got_out = collect(out_even, out_odd, n)
    dqkv, q_even, q_odd, kv_even, kv_odd, grad_norm1 = call(
        functools.partial(attend_back_kernel, n, heads),
        [((count, qkv_cols), BF)] + [((n // 2, chunk, q_cols), BF)] * 2
        + [((n // 2, chunk, 2 * kv_cols), BF)] * 2 + [((8, D), F32)],
        [pltpu.VMEM((D, qkv_cols), BF), dma((n,))],
        [SMEM] * 2 + [ANY] * n + [VMEM] * 4,
        [owners, me, *attn_w, n1, qkv, do, bias],
        8e9, 5e6,
    )
    sum_q = total(list(collect(q_even, q_odd, n).values()))
    sum_kv = total(list(collect(kv_even, kv_odd, n).values()))
    part = call(
        functools.partial(input_grad_kernel, n),
        [block] * 4,
        [pltpu.VMEM((D, qkv_cols), BF), dma((n,))],
        [SMEM] + [ANY] * n + [VMEM],
        [owners, *attn_w, dqkv],
        1e9, 6e6,
    )
    got_down, got_gate, got_up, got_out, _ = lax.optimization_barrier(
        (got_down, got_gate, got_up, got_out, part[0])
    )
    sum_down = jnp.swapaxes(share(got_down), 1, 2)
    sum_gate, sum_up = share(got_gate), share(got_up)
    sum_out = total(list(got_out.values())).T
    (grad_input,) = call(
        input_kernel, [((own, D), F32)], [], [VMEM] * 6,
        [x_own, *seq_scatter(part), dh, small], 0, 3e6,
    )
    y_parts = wide_scatter(y_near, y_away)
    layer_out = total([h, y_parts[0][0], y_parts[1][0], *y_parts[2:]]).astype(BF)

    tiny = jnp.concatenate([grad_norm1[:1], grad_norm2, grad_router[:4], jnp.zeros((2, D), F32)], axis=0)
    for bit in range(n.bit_length() - 1):
        tiny = tiny + move(tiny, "fsdp", 1 << bit)
    tiny = lax.dynamic_slice_in_dim(tiny, mine * chunk, chunk, axis=1)
    for bit in (2, 1):
        tiny = tiny + move(tiny, "seq", bit)

    lead = (micro, 1, rows, D)
    return (
        layer_out.reshape(lead),
        grad_input.reshape(lead),
        tiny[0] / norm1.astype(F32),
        sum_q,
        sum_kv[:, :kv_cols],
        sum_kv[:, kv_cols:],
        sum_out,
        tiny[1],
        tiny[2:6].T,
        sum_gate,
        sum_up,
        sum_down,
    )


def solution(mesh):
    return jax.shard_map(
        on_device,
        mesh=mesh,
        in_specs=(
            P(None, "fsdp", "seq", None),
            P(None, "fsdp", None),
            P(None, "fsdp", None, None),
            P(None, "fsdp", "seq", None),
            P("fsdp"),
            P("fsdp", "seq"),
            P("fsdp", "seq"),
            P("fsdp", "seq"),
            P("seq", "fsdp"),
            P("fsdp"),
            P("fsdp", None),
            P(None, "fsdp", "seq"),
            P(None, "fsdp", "seq"),
            P(None, "seq", "fsdp"),
        ),
        out_specs=(
            P(None, "fsdp", "seq", None),
            P(None, "fsdp", "seq", None),
            P("fsdp"),
            P("fsdp", "seq"),
            P("fsdp", "seq"),
            P("fsdp", "seq"),
            P("seq", "fsdp"),
            P("fsdp"),
            P("fsdp", None),
            P(None, "fsdp", "seq"),
            P(None, "fsdp", "seq"),
            P(None, "seq", "fsdp"),
        ),
        check_vma=False,
    )
```

```python
import functools

import jax
import jax.numpy as jnp
from jax import lax
from jax.experimental import pallas as pl
from jax.experimental.pallas import tpu as pltpu
from jax.sharding import PartitionSpec as P


D = 1536
HEADS = 24
HEAD_DIM = 64
KV_HEADS = 8
EXPERTS = 4
GROUP = HEADS // KV_HEADS
SCALE = HEAD_DIM**-0.5
EPS = 1e-05
NEG = -1e30
BF = jnp.bfloat16
F32 = jnp.float32
LANES = 128
EXTRA = 16
PAIR = 2
TILE = 384

VMEM = pl.BlockSpec(memory_space=pltpu.VMEM)
SMEM = pl.BlockSpec(memory_space=pltpu.SMEM)
ANY = pl.BlockSpec(memory_space=pl.ANY)


def mm(a, b, dims=((1,), (0,))):
    return lax.dot_general(a, b, (dims, ((), ())), preferred_element_type=F32)


def move(value, axis, bit):
    return lax.ppermute(value, axis, [(i, i ^ bit) for i in range(lax.axis_size(axis))])


def move_both(value, seq_bit, fsdp_bit):
    n = lax.axis_size("fsdp")
    pairs = [
        (s * n + f, (s ^ seq_bit) * n + (f ^ fsdp_bit))
        for s in range(lax.axis_size("seq"))
        for f in range(n)
    ]
    return lax.ppermute(value, ("seq", "fsdp"), pairs)


def spread(mine, other, n):
    units = [None] * n
    units[0] = mine
    for d in directions(n):
        units[d] = move(other if d & PAIR else mine, "fsdp", d)
    for d in range(0, n, 2):
        units[d ^ 1] = move(units[d], "fsdp", 1)
    return units


def collect(even, odd, n):
    odd = move(odd, "fsdp", 1)
    sums = [even[i].astype(F32) + odd[i].astype(F32) for i in range(n // 2)]
    got = {0: sums[0]}
    for i in range(n // 2 - 1, 0, -1):
        got[2 * i] = move(sums[i].astype(BF), "fsdp", 2 * i)
    return got


def total(parts):
    out = parts[0].astype(F32)
    for part in parts[1:]:
        out = out + part.astype(F32)
    return out


def add(a, b):
    return (a.astype(F32) + b.astype(F32)).astype(BF)


def seq_gather(block):
    second = move(block, "seq", 2)
    first = move(block, "seq", 1)
    third = move(second, "seq", 1)
    return [block, first, second, third]


def seq_scatter(terms):
    third = move(terms[3], "seq", 1)
    second = move(add(terms[2], third), "seq", 2)
    first = move(terms[1], "seq", 1)
    return [terms[0], first, second]


BLOCKS = ((0, 0), (2, 0), (0, PAIR), (2, PAIR), (1, 0), (3, 0), (1, PAIR), (3, PAIR))


def wide_gather(block):
    pair = move(block, "fsdp", PAIR)
    far = move(block, "seq", 2)
    both = move(pair, "seq", 2)
    near = [block, far, pair, both]
    return near + [move(b, "seq", 1) for b in near]


def wide_scatter(near, away):
    away = move(away, "seq", 1)
    both = move_both(add(near[3], away[3]), 2, PAIR)
    pair = move(add(near[2], away[2]), "fsdp", PAIR)
    far = move(add(near[1], away[1]), "seq", 2)
    return [near, away, far, pair, both]


def call(kernel, outs, scratch, specs, args, flops, moved, out_specs=None, grid=()):
    return pl.pallas_call(
        kernel,
        grid=grid,
        in_specs=specs,
        out_specs=out_specs or [VMEM] * len(outs),
        out_shape=[jax.ShapeDtypeStruct(s, d) for s, d in outs],
        scratch_shapes=scratch,
        compiler_params=pltpu.CompilerParams(vmem_limit_bytes=56 * 2**20),
        cost_estimate=pl.CostEstimate(
            flops=int(flops), bytes_accessed=int(moved), transcendentals=0
        ),
    )(*args)


def normal(v):
    return v * lax.rsqrt(jnp.mean(v * v, axis=-1, keepdims=True) + EPS)


def rows_of(owners, k, rows):
    return pl.ds(pl.multiple_of(owners[k] * rows, 16), rows)


def slab(j, per, micro, rows):
    return pl.ds(pl.multiple_of(j * per + micro * rows, rows), rows)


def slabs(ref, micro, rows):
    per = ref.shape[0] // 4
    return jnp.concatenate([ref[slab(j, per, micro, rows)] for j in range(4)], axis=0)


def softmax(query, key, bias):
    scores = mm(query, key, ((1,), (1,))) + bias
    raised = jnp.exp(scores - jnp.max(scores, axis=-1, keepdims=True))
    return raised * (1.0 / jnp.sum(raised, axis=-1, keepdims=True))


def attn_pack_kernel(q_ref, k_ref, v_ref, one_ref, two_ref, router_ref, out_ref):
    chunk, at = q_ref.shape[0], 0
    for ref in (q_ref, k_ref, v_ref):
        out_ref[:chunk, at : at + ref.shape[1]] = ref[...]
        at += ref.shape[1]
    rest = jnp.zeros((EXTRA - 2 - EXPERTS, chunk), F32)
    small = [one_ref[...].reshape(1, chunk), two_ref[...].reshape(1, chunk), router_ref[...]]
    out_ref[chunk:, :chunk] = jnp.concatenate([v.astype(F32) for v in small] + [rest], axis=0).astype(BF)


def expert_pack_kernel(side, gate_ref, up_ref, down_ref, mine_ref, other_ref):
    hidden = gate_ref.shape[2] // 2
    wide = EXPERTS * hidden
    for e in range(EXPERTS):
        down = down_ref[e]
        for half in range(2):
            at = slice(half * hidden, (half + 1) * hidden)
            to = slice(e * hidden, (e + 1) * hidden)

            def put(ref):
                ref[:, to] = gate_ref[e, :, at]
                ref[:, slice(wide + to.start, wide + to.stop)] = up_ref[e, :, at]
                ref[:, slice(2 * wide + to.start, 2 * wide + to.stop)] = down[:, at]

            pl.when(side[0] == half)(functools.partial(put, mine_ref))
            pl.when(side[0] != half)(functools.partial(put, other_ref))


def norm_kernel(x_ref, a_ref, b_ref, c_ref, gain_ref, h_ref, n_ref):
    h = total([x_ref[...], a_ref[...], b_ref[...], c_ref[...]])
    h_ref[...] = h
    n_ref[...] = (normal(h) * gain_ref[1:2]).astype(BF)


def norm_back(v, gain, upstream):
    factor = lax.rsqrt(jnp.mean(v * v, axis=-1, keepdims=True) + EPS)
    normed = v * factor
    scaled = upstream * gain
    back = factor * (scaled - normed * jnp.mean(scaled * normed, axis=-1, keepdims=True))
    return back, jnp.sum(upstream * normed, axis=0, keepdims=True)


def norm_back_kernel(near_ref, away_ref, a_ref, b_ref, c_ref, h_ref, dy_ref, gain_ref, dh_ref, da_ref, g_ref):
    dn2 = total([near_ref[0], away_ref[0], a_ref[...], b_ref[...], c_ref[...]])
    back, grad = norm_back(h_ref[...], gain_ref[1:2], dn2)
    dh = dy_ref[...].astype(F32) + back
    dh_ref[...] = dh
    da_ref[...] = dh.astype(BF)
    g_ref[...] = grad


def input_kernel(x_ref, a_ref, b_ref, c_ref, dh_ref, gain_ref, out_ref):
    dn1 = total([a_ref[...], b_ref[...], c_ref[...]])
    out_ref[...] = dh_ref[...] + norm_back(x_ref[...].astype(F32), gain_ref[0:1], dn1)[0]


def fetch(pieces, owners, whole, sem, rows, columns=slice(None)):
    copies = [
        pltpu.make_async_copy(piece.at[:rows, columns], whole.at[rows_of(owners, k, rows)], sem.at[k])
        for k, piece in enumerate(pieces)
    ]
    for copy in copies:
        copy.start()
    return copies


def wait(copies):
    for copy in copies:
        copy.wait()


def qkv_kernel(n, owners, *refs):
    x_refs, pieces, refs = refs[:4], refs[4 : 4 + n], refs[4 + n :]
    n1_ref, qkv_ref, small_ref, w, extra, sem, small_sem = refs
    chunk = D // n
    smalls = [
        pltpu.make_async_copy(piece.at[chunk:, : extra.shape[2]], extra.at[owners[k]], small_sem.at[k])
        for k, piece in enumerate(pieces)
    ]
    for copy in smalls:
        copy.start()
    copies = fetch(pieces, owners, w, sem, chunk)
    wait(smalls)
    small = jnp.concatenate([extra[j].astype(F32)[:, :chunk] for j in range(n)], axis=1)
    small_ref[...] = small
    gain = small[0:1]
    block = x_refs[0].shape[0]
    for j in range(4):
        n1_ref[j * block : (j + 1) * block] = (normal(x_refs[j][...].astype(F32)) * gain).astype(BF)
    wait(copies)
    qkv_ref[...] = mm(n1_ref[...], w[...]).astype(BF)


def attend_kernel(n, heads, owners, *refs):
    pieces, (qkv_ref, bias_ref, mix_ref, probs_ref, *part_refs, w, sem) = refs[:n], refs[n:]
    copies = fetch(pieces, owners, w, sem, D // n)
    q_cols = heads * HEAD_DIM
    kv_cols = q_cols // GROUP
    micro, rows = bias_ref.shape[0], bias_ref.shape[1] // 4
    block = qkv_ref.shape[0] // 4

    def sequence(m, carry):
        qkv = slabs(qkv_ref, m, rows)
        bias = bias_ref[m]
        mixed = []
        for head in range(heads):
            kv = head // GROUP
            key = qkv[:, q_cols + kv * HEAD_DIM : q_cols + (kv + 1) * HEAD_DIM]
            value = qkv[:, q_cols + kv_cols + kv * HEAD_DIM : q_cols + kv_cols + (kv + 1) * HEAD_DIM]
            query = qkv[:, head * HEAD_DIM : (head + 1) * HEAD_DIM] * BF(SCALE)
            probs = softmax(query, key, bias).astype(BF)
            probs_ref[m * heads + head] = probs
            mixed.append(mm(probs, value).astype(BF))
        mixed = jnp.concatenate(mixed, axis=1)
        for j in range(4):
            mix_ref[slab(j, block, m, rows)] = mixed[j * rows : (j + 1) * rows]
        return carry

    lax.fori_loop(0, micro, sequence, 0)
    wait(copies)
    part = mm(mix_ref[...], w[...], ((1,), (1,))).astype(BF)
    for j in range(4):
        part_refs[j][...] = part[j * block : (j + 1) * block]


def store_units(even_ref, odd_ref, mine, first, value):
    rows = D // (2 * even_ref.shape[0])
    flag = (mine & 1) == 1
    for i in range(value.shape[0] // (2 * rows)):
        a = value[2 * i * rows : (2 * i + 1) * rows]
        b = value[(2 * i + 1) * rows : (2 * i + 2) * rows]
        slot = (mine >> 1) ^ (first + i)
        even_ref[slot, :rows] = jnp.where(flag, b, a).astype(BF)
        odd_ref[slot, :rows] = jnp.where(flag, a, b).astype(BF)


def tiles(rows, body):
    per = TILE // (2 * rows)

    def step(i, carry):
        body(pl.ds(pl.multiple_of(i * TILE, TILE), TILE), i * per)
        return carry

    lax.fori_loop(0, D // TILE, step, 0)


def out_back_kernel(n, owners, mine, *refs):
    da_refs, pieces, refs = refs[:4], refs[4 : 4 + n], refs[4 + n :]
    mix_ref, do_ref, even_ref, odd_ref, w, da_all, sem = refs
    chunk = D // n
    copies = fetch(pieces, owners, w, sem, chunk)
    block = da_refs[0].shape[0]
    for j in range(4):
        da_all[j * block : (j + 1) * block] = da_refs[j][...]

    def grads(at, first):
        store_units(even_ref, odd_ref, mine[0], first, mm(da_all[:, at], mix_ref[...], ((0,), (0,))))

    tiles(chunk, grads)
    wait(copies)
    do_ref[...] = mm(da_all[...], w[...]).astype(BF)


def attend_back_kernel(n, heads, owners, mine, *refs):
    pieces, refs = refs[:n], refs[n:]
    n1_ref, qkv_ref, do_ref, probs_ref, norm2_ref, router_ref, d_ref, *unit_refs, w, sem = refs
    chunk, cols = D // n, w.shape[1]
    copies = fetch(pieces, owners, w, sem, chunk)
    q_cols = heads * HEAD_DIM
    kv_cols = q_cols // GROUP
    block = n1_ref.shape[0] // 4
    length = probs_ref.shape[1]
    rows, micro = length // 4, probs_ref.shape[0] // heads

    def sequence(m, carry):
        qkv = slabs(qkv_ref, m, rows)
        grad = slabs(do_ref, m, rows)
        grad_query, grad_key, grad_value = [], [], []
        for kv in range(heads // GROUP):
            key = qkv[:, q_cols + kv * HEAD_DIM : q_cols + (kv + 1) * HEAD_DIM] * BF(SCALE)
            value = qkv[:, q_cols + kv_cols + kv * HEAD_DIM : q_cols + kv_cols + (kv + 1) * HEAD_DIM]
            sum_key = jnp.zeros((length, HEAD_DIM), F32)
            sum_value = jnp.zeros((length, HEAD_DIM), F32)
            for head in range(kv * GROUP, (kv + 1) * GROUP):
                query = qkv[:, head * HEAD_DIM : (head + 1) * HEAD_DIM] * BF(SCALE)
                upstream = grad[:, head * HEAD_DIM : (head + 1) * HEAD_DIM]
                low = probs_ref[m * heads + head]
                probs = low.astype(F32)
                dp = mm(upstream, value, ((1,), (1,)))
                ds = (probs * (dp - jnp.sum(dp * probs, axis=-1, keepdims=True))).astype(BF)
                grad_query.append(mm(ds, key).astype(BF))
                sum_key += mm(ds, query, ((0,), (0,)))
                sum_value += mm(low, upstream, ((0,), (0,)))
            grad_key.append(sum_key.astype(BF))
            grad_value.append(sum_value.astype(BF))
        whole = jnp.concatenate(grad_query + grad_key + grad_value, axis=1)
        for j in range(4):
            d_ref[slab(j, block, m, rows)] = whole[j * rows : (j + 1) * rows]
        return carry

    lax.fori_loop(0, micro, sequence, 0)
    wait(copies)
    ones = jnp.ones((8, 2 * cols), BF)
    q_even, q_odd, kv_even, kv_odd = unit_refs
    flag = (mine[0] & 1) == 1

    def grads(at, first):
        value = mm(n1_ref[:, at], d_ref[...], ((0,), (0,)))
        store_units(q_even, q_odd, mine[0], first, value[:, :q_cols])
        store_units(kv_even, kv_odd, mine[0], first, value[:, q_cols:])
        gain = mm(ones, split(value * w[at].astype(F32)), ((1,), (1,)))
        small = [gain[:1], norm2_ref[:, at], router_ref[:EXPERTS, at]]
        small.append(jnp.zeros((EXTRA - 2 - EXPERTS, TILE), F32))
        small = jnp.concatenate(small, axis=0)
        pad = jnp.zeros((EXTRA, q_cols - chunk), F32)
        for i in range(TILE // (2 * chunk)):
            a = small[:, 2 * i * chunk : (2 * i + 1) * chunk]
            b = small[:, (2 * i + 1) * chunk : (2 * i + 2) * chunk]
            slot = (mine[0] >> 1) ^ (first + i)
            q_even[slot, chunk:] = jnp.concatenate([jnp.where(flag, b, a), pad], axis=1).astype(BF)
            q_odd[slot, chunk:] = jnp.concatenate([jnp.where(flag, a, b), pad], axis=1).astype(BF)

    tiles(chunk, grads)


def input_grad_kernel(n, owners, *refs):
    pieces, refs = refs[:n], refs[n:]
    d_ref, *refs = refs
    part_refs, (w, sem) = refs[:4], refs[4:]
    wait(fetch(pieces, owners, w, sem, D // n))
    block = part_refs[0].shape[0]
    part = mm(d_ref[...], w[...], ((1,), (1,))).astype(BF)
    for j in range(4):
        part_refs[j][...] = part[j * block : (j + 1) * block]


def split(v):
    high = v.astype(BF)
    return jnp.concatenate([high, (v - high.astype(F32)).astype(BF)], axis=1)


ROWS = 256


def expert_kernel(n, owners, mine, *refs):
    n2_refs, dy_refs, pieces, refs = refs[:8], refs[8:16], refs[16 : 16 + n], refs[16 + n :]
    router_ref, chosen_ref, zg_out, dgu_out, near_out, away_out, even_ref, odd_ref, *refs = refs
    w, n2_all, dy_all, chosen_all, zg, dgu, part, wsem, tsem, csem, osem = refs
    count, wide = zg.shape
    block = n2_refs[0].shape[0]
    chunk = D // n
    per = ROWS // block
    steps = count // ROWS
    cut = 2 * wide + LANES

    def tile(i):
        return pl.ds(pl.multiple_of(i * ROWS, ROWS), ROWS)

    first = [pltpu.make_async_copy(router_ref, w.at[:, 2 * wide : cut], csem.at[0])]
    second = []
    for k, piece in enumerate(pieces):
        at = rows_of(owners, k, chunk)
        first.append(pltpu.make_async_copy(piece.at[:, : 2 * wide], w.at[at, : 2 * wide], wsem.at[0, k]))
        second.append(pltpu.make_async_copy(piece.at[:, 2 * wide :], w.at[at, cut:], wsem.at[1, k]))
    tokens = []
    for k in range(len(n2_refs)):
        at = pl.ds(k * block, block)
        tokens.append(pltpu.make_async_copy(n2_refs[k], n2_all.at[at], tsem.at[0, k // per]))
        tokens.append(pltpu.make_async_copy(dy_refs[k], dy_all.at[at], tsem.at[1, k // per]))
    masks = pltpu.make_async_copy(chosen_ref, chosen_all, csem.at[1])
    for copy in first + tokens[: 2 * per] + [masks] + second:
        copy.start()
    for copy in first + [masks] + second:
        copy.wait()
    for copy in tokens[2 * per :]:
        copy.start()
    lane = lax.broadcasted_iota(jnp.int32, (LANES, wide), 0)
    column = lax.broadcasted_iota(jnp.int32, (LANES, wide), 1)
    expand = (lane == column // (wide // EXPERTS)).astype(BF)
    expand_two = jnp.concatenate([expand, expand], axis=0)

    half = steps // 2

    def row_copies(i):
        return [
            pltpu.make_async_copy(zg.at[tile(i)], zg_out.at[tile(i)], osem.at[0, i]),
            pltpu.make_async_copy(dgu.at[tile(i)], dgu_out.at[tile(i)], osem.at[1, i]),
        ]

    def part_copy(i, out, start):
        return pltpu.make_async_copy(
            part.at[pl.ds(i * per, per)], out.at[pl.ds(i * per - start, per)], osem.at[2, i]
        )

    def step(i, carry):
        at = tile(i)
        for which, ref in enumerate((n2_all, dy_all)):
            pltpu.make_async_copy(ref.at[at], ref.at[at], tsem.at[which, i]).wait()
        chosen = chosen_all[at] > 0
        big = mm(n2_all[at], w[:, :cut])
        dz = mm(dy_all[at], w[:, cut:])
        g, u = big[:, :wide], big[:, wide : 2 * wide]
        logits = jnp.where(chosen, big[:, 2 * wide :], 0.0)
        other = jnp.sum(logits, axis=-1, keepdims=True) - logits
        gating = jnp.where(chosen, 1.0 / (1.0 + jnp.exp(other - logits)), 0.0)
        weight = mm(split(gating), expand_two)
        sig = 0.5 * jnp.tanh(0.5 * g) + 0.5
        act = g * sig
        z = act * u
        zg[at] = (z * weight).astype(BF)
        dgate = jnp.where(chosen, mm((z * dz).astype(BF), expand, ((1,), (1,))), 0.0)
        dz = dz * weight
        dgu[at, :wide] = (dz * u * (sig + act * (1.0 - sig))).astype(BF)
        dgu[at, wide : 2 * wide] = (dz * act).astype(BF)
        dlogits = gating * (dgate - jnp.sum(gating * dgate, axis=-1, keepdims=True))
        dgu[at, 2 * wide :] = dlogits.astype(BF)
        dn2 = mm(dgu[at], w[:, :cut], ((1,), (1,)))
        for b in range(per):
            part[i * per + b] = dn2[b * block : (b + 1) * block].astype(BF)
        for copy in row_copies(i):
            copy.start()
        pl.when(i < half)(lambda: part_copy(i, near_out, 0).start())
        pl.when(i >= half)(lambda: part_copy(i, away_out, half * per).start())
        return carry

    lax.fori_loop(0, steps, step, 0)

    def grads(at, first):
        store_units(even_ref, odd_ref, mine[0], first, mm(dy_all[:, at], zg[...], ((0,), (0,))))

    tiles(chunk, grads)
    for i in range(steps):
        for copy in row_copies(i):
            copy.wait()
        (part_copy(i, near_out, 0) if i < half else part_copy(i, away_out, half * per)).wait()


def gate_grad_kernel(n, mine, *refs):
    n2_refs, refs = refs[:8], refs[8:]
    dgu_ref, gate_even, gate_odd, up_even, up_odd, router_ref, n2_all, sem = refs
    block = n2_refs[0].shape[0]
    copies = [
        pltpu.make_async_copy(ref, n2_all.at[pl.ds(k * block, block)], sem.at[k])
        for k, ref in enumerate(n2_refs)
    ]
    for copy in copies:
        copy.start()
    for copy in copies:
        copy.wait()
    wide = gate_even.shape[2]

    def grads(at, first):
        value = mm(n2_all[:, at], dgu_ref[...], ((0,), (0,)))
        store_units(gate_even, gate_odd, mine[0], first, value[:, :wide])
        store_units(up_even, up_odd, mine[0], first, value[:, wide : 2 * wide])
        router_ref[:, at] = value[:, 2 * wide :].T[:8]

    tiles(D // n, grads)


def expert_out_kernel(n, owners, *refs):
    pieces, (zg_ref, near_ref, away_ref, w, sem) = refs[:n], refs[n:]
    wide = zg_ref.shape[1]
    chunk = D // n
    wait(fetch(pieces, owners, w, sem, chunk, slice(2 * wide, 3 * wide)))
    block = near_ref.shape[1]
    for h, ref in enumerate((near_ref, away_ref)):
        value = mm(zg_ref[pl.ds(h * 4 * block, 4 * block)], w[...], ((1,), (1,)))
        ref[...] = value.astype(BF).reshape(4, block, D)


def finish_kernel(counts, hidden, side, *refs):
    ins, outs = refs[: sum(counts)], refs[sum(counts) :]
    first = side[0] == 0
    for count, out in zip(counts[:-1], outs):
        here, ins = ins[:count], ins[count:]
        near = total([ref[...] for ref in here[: count // 2]])
        pair = total([ref[...] for ref in here[count // 2 :]])
        for e in range(EXPERTS):
            at = slice(e * hidden, (e + 1) * hidden)
            out[e, :, :hidden] = jnp.where(first, near[:, at], pair[:, at])
            out[e, :, hidden:] = jnp.where(first, pair[:, at], near[:, at])
    outs[-1][...] = total([ref[...] for ref in ins])


def on_device(
    tokens, segments, routes, cotangent, norm1, w_query, w_key, w_value, w_out,
    norm2, w_router, w_gate, w_up, w_down,
):
    seq = lax.axis_index("seq")
    mine = lax.axis_index("fsdp")
    n = lax.axis_size("fsdp")
    parts = lax.axis_size("seq")
    owners = (mine ^ jnp.arange(n, dtype=jnp.int32)).astype(jnp.int32)
    me = mine.reshape(1).astype(jnp.int32)
    side = jnp.where(mine & PAIR, 1, 0)
    micro, rows = tokens.shape[0], tokens.shape[2]
    own = micro * rows
    count = parts * own
    chunk = w_query.shape[0]
    q_cols, kv_cols = w_query.shape[1], w_key.shape[1]
    qkv_cols = q_cols + 2 * kv_cols
    heads = q_cols // HEAD_DIM
    hidden = w_gate.shape[2] // 2
    wide = EXPERTS * hidden

    (attn,) = call(
        attn_pack_kernel, [((chunk + EXTRA, qkv_cols), BF)], [], [VMEM] * 6,
        [w_query, w_key, w_value, norm1, norm2, w_router.T], 0, 1e6,
    )
    qkv_w = spread(attn, attn, n)
    out_w = spread(w_out.T, w_out.T, n)
    x_own = tokens.reshape(own, D)
    dy_own = cotangent.reshape(own, D)
    x_all = seq_gather(x_own)

    here, there = call(
        expert_pack_kernel, [((chunk, 3 * wide), BF)] * 2, [], [SMEM] + [VMEM] * 3,
        [side.reshape(1).astype(jnp.int32), w_gate, w_up, jnp.swapaxes(w_down, 1, 2)], 0, 3e6,
    )
    expert_w = spread(here, there, n)
    dy_all = wide_gather(dy_own)

    ids = seq ^ jnp.arange(parts, dtype=jnp.int32)
    places = (ids[:, None] * rows + jnp.arange(rows, dtype=jnp.int32)[None]).reshape(-1)
    seg = jnp.take(segments[:, 0].reshape(micro, parts, rows), ids, axis=1).reshape(micro, -1)
    allowed = (seg[:, :, None] == seg[:, None, :]) & (places[None, None, :] <= places[None, :, None])
    bias = jnp.where(allowed, 0.0, NEG).astype(F32)
    here = routes[:, 0].reshape(-1, LANES)
    both = jnp.stack([here, move(here, "fsdp", PAIR)]).reshape(2, micro, parts, rows, 2)
    route = jnp.stack([both[1 if k else 0][:, seq ^ j] for j, k in BLOCKS]).reshape(-1, 2)
    lane = jnp.arange(LANES, dtype=jnp.int32)
    chosen = ((route[:, :1] == lane) | (route[:, 1:] == lane)).astype(F32)

    dma = pltpu.SemaphoreType.DMA
    block = ((own, D), BF)
    n1, qkv, small = call(
        functools.partial(qkv_kernel, n),
        [((count, D), BF), ((count, qkv_cols), BF), ((EXTRA, D), F32)],
        [pltpu.VMEM((D, qkv_cols), BF), pltpu.VMEM((n, EXTRA, 2 * LANES), BF), dma((n,)), dma((n,))],
        [SMEM] + [VMEM] * 4 + [ANY] * n,
        [owners, *x_all, *qkv_w],
        1e9, 6e6,
    )
    length = parts * rows
    mixed, probs, *part = call(
        functools.partial(attend_kernel, n, heads),
        [((count, q_cols), BF), ((micro * heads, length, length), BF)] + [block] * 4,
        [pltpu.VMEM((D, q_cols), BF), dma((n,))],
        [SMEM] + [ANY] * n + [VMEM] * 2, [owners, *out_w, qkv, bias], 5e9, 6e6,
    )

    router = jnp.pad(small[2:6].astype(BF), ((0, LANES - 4), (0, 0))).T
    h, n2_own = call(
        norm_kernel, [((own, D), F32), block], [], [VMEM] * 5,
        [x_own, *seq_scatter(part), small], 0, 3e6,
    )
    n2_all = wide_gather(n2_own)
    span = len(BLOCKS) * own
    four = ((4, own, D), BF)
    units = ((n // 2, chunk, wide), BF)
    zg, dgu, near, away, down_even, down_odd = call(
        functools.partial(expert_kernel, n),
        [((span, wide), BF), ((span, 2 * wide + LANES), BF), four, four, units, units],
        [
            pltpu.VMEM((D, 3 * wide + LANES), BF), pltpu.VMEM((span, D), BF), pltpu.VMEM((span, D), BF),
            pltpu.VMEM((span, LANES), F32), pltpu.VMEM((span, wide), BF),
            pltpu.VMEM((span, 2 * wide + LANES), BF), pltpu.VMEM((len(BLOCKS), own, D), BF),
            dma((2, n)), dma((2, span // ROWS)), dma((2,)), dma((3, span // ROWS)),
        ],
        [SMEM] * 2 + [ANY] * (18 + n),
        [owners, me, *n2_all, *dy_all, *expert_w, router, chosen],
        1e10, 2e7, [ANY] * 4 + [VMEM] * 2,
    )
    dn2 = wide_scatter(near, away)
    gate_even, gate_odd, up_even, up_odd, grad_router = call(
        functools.partial(gate_grad_kernel, n),
        [units] * 4 + [((8, D), F32)],
        [pltpu.VMEM((span, D), BF), dma((len(BLOCKS),))],
        [SMEM] + [ANY] * 8 + [VMEM],
        [me, *n2_all, dgu],
        3.5e9, 9e6,
    )

    got_down = collect(down_even, down_odd, n)
    got_gate = collect(gate_even, gate_odd, n)
    got_up = collect(up_even, up_odd, n)

    corner = pl.BlockSpec((1, own, D), lambda i: (0, 0, 0))
    dh, da, grad_norm2 = call(
        norm_back_kernel, [((own, D), F32), block, ((1, D), F32)], [], [corner] * 2 + [VMEM] * 6,
        [*dn2, h, dy_own, small], 0, 5e6, grid=(1,),
    )

    da = seq_gather(da)
    y_near, y_away = call(
        functools.partial(expert_out_kernel, n),
        [four, four],
        [pltpu.VMEM((D, wide), BF), dma((n,))],
        [SMEM] + [ANY] * n + [VMEM],
        [owners, *expert_w, zg],
        1.6e9, 6e6,
    )
    do, out_even, out_odd = call(
        functools.partial(out_back_kernel, n),
        [((count, q_cols), BF), ((n // 2, chunk, q_cols), BF), ((n // 2, chunk, q_cols), BF)],
        [pltpu.VMEM((D, q_cols), BF), pltpu.VMEM((count, D), BF), dma((n,))],
        [SMEM] * 2 + [VMEM] * 4 + [ANY] * n + [VMEM],
        [owners, me, *da, *out_w, mixed],
        1.2e9, 4e6,
    )
    got_out = collect(out_even, out_odd, n)
    dqkv, q_even, q_odd, kv_even, kv_odd = call(
        functools.partial(attend_back_kernel, n, heads),
        [((count, qkv_cols), BF)] + [((n // 2, chunk + EXTRA, q_cols), BF)] * 2
        + [((n // 2, chunk, 2 * kv_cols), BF)] * 2,
        [pltpu.VMEM((D, qkv_cols), BF), dma((n,))],
        [SMEM] * 2 + [ANY] * n + [VMEM] * 6,
        [owners, me, *qkv_w, n1, qkv, do, probs, grad_norm2, grad_router],
        8e9, 5e6,
    )
    sum_q = total(list(collect(q_even, q_odd, n).values()))
    sum_kv = total(list(collect(kv_even, kv_odd, n).values()))
    part = call(
        functools.partial(input_grad_kernel, n),
        [block] * 4,
        [pltpu.VMEM((D, qkv_cols), BF), dma((n,))],
        [SMEM] + [ANY] * n + [VMEM],
        [owners, *qkv_w, dqkv],
        1e9, 6e6,
    )
    (grad_input,) = call(
        input_kernel, [((own, D), F32)], [], [VMEM] * 6,
        [x_own, *seq_scatter(part), dh, small], 0, 3e6,
    )
    ins = []
    for got in (got_down, got_gate, got_up):
        ins.append([got[d] for d in got if not d & PAIR] + [got[d] for d in got if d & PAIR])
    ins.append(list(got_out.values()))
    sum_down, sum_gate, sum_up, sum_out = call(
        functools.partial(finish_kernel, [len(v) for v in ins], hidden),
        [((EXPERTS, chunk, 2 * hidden), F32)] * 3 + [((chunk, q_cols), F32)], [],
        [SMEM] + [VMEM] * sum(len(v) for v in ins),
        [side.reshape(1).astype(jnp.int32)] + [v for part in ins for v in part], 0, 6e6,
    )
    y_away = move(y_away, "seq", 1)
    far = move(add(y_near[1::2], y_away[1::2]), "seq", 2)
    pair = move(total([y_near[2], y_away[2], far[1]]).astype(BF), "fsdp", PAIR)
    layer_out = total([h, y_near[0], y_away[0], far[0], pair]).astype(BF)

    tiny = sum_q[chunk : chunk + 8, :chunk]
    tiny = tiny + move(tiny, "seq", 2)
    tiny = tiny + move(tiny, "seq", 1)

    lead = (micro, 1, rows, D)
    return (
        layer_out.reshape(lead),
        grad_input.reshape(lead),
        tiny[0] / norm1.astype(F32),
        sum_q[:chunk],
        sum_kv[:, :kv_cols],
        sum_kv[:, kv_cols:],
        sum_out.T,
        tiny[1],
        tiny[2:6].T,
        sum_gate,
        sum_up,
        jnp.swapaxes(sum_down, 1, 2),
    )


def directions(n):
    return sorted(range(2, n, 2), key=lambda d: (d & (d - 1) != 0, -d))


def solution(mesh):
    return jax.shard_map(
        on_device,
        mesh=mesh,
        in_specs=(
            P(None, "fsdp", "seq", None),
            P(None, "fsdp", None),
            P(None, "fsdp", None, None),
            P(None, "fsdp", "seq", None),
            P("fsdp"),
            P("fsdp", "seq"),
            P("fsdp", "seq"),
            P("fsdp", "seq"),
            P("seq", "fsdp"),
            P("fsdp"),
            P("fsdp", None),
            P(None, "fsdp", "seq"),
            P(None, "fsdp", "seq"),
            P(None, "seq", "fsdp"),
        ),
        out_specs=(
            P(None, "fsdp", "seq", None),
            P(None, "fsdp", "seq", None),
            P("fsdp"),
            P("fsdp", "seq"),
            P("fsdp", "seq"),
            P("fsdp", "seq"),
            P("seq", "fsdp"),
            P("fsdp"),
            P("fsdp", None),
            P(None, "fsdp", "seq"),
            P(None, "fsdp", "seq"),
            P(None, "seq", "fsdp"),
        ),
        check_vma=False,
    )
```
